32 devices in a mesh: dp: 4 (over y, x), row: 2 (over core), col: 4 (over z).
Axes of the slice: x: 2, y: 2, z: 4, core: 2. Of those that a mesh axis runs over, the one named last changes fastest.
Arguments:
- block_input: bfloat16 [2048, 1024], P(('dp', 'row'), 'col'), may hold values from -6 to 6
- norm1_gain: float32 [1024], P('col'), may hold values from 0.1 to 1.9
- query_weight: bfloat16 [1024, 1024], P('col', 'row'), may hold values from -0.1875 to 0.1875
- key_weight: bfloat16 [1024, 512], P('col', 'row'), may hold values from -0.1875 to 0.1875
- value_weight: bfloat16 [1024, 512], P('col', 'row'), may hold values from -0.1875 to 0.1875
- query_gain: float32 [64], replicated, may hold values from 0.1 to 1.9
- key_gain: float32 [64], replicated, may hold values from 0.1 to 1.9
- output_weight: bfloat16 [1024, 1024], P('row', 'col'), may hold values from -0.75 to 0.75
- norm2_gain: float32 [1024], P('col'), may hold values from 0.1 to 1.9
- w_gate: bfloat16 [1024, 4608], P('col', 'row'), may hold values from -0.1875 to 0.1875
- w_up: bfloat16 [1024, 4608], P('col', 'row'), may hold values from -0.1875 to 0.1875
- w_down: bfloat16 [4608, 1024], P('row', 'col'), may hold values from -0.09375 to 0.09375
- segments: int32 [2048], P('dp'), may hold values from 0 to 5, never falling along the last dimension, each value on 1 to 1024 neighbouring positions
- positions: int32 [2048], P('dp'), may hold values from 0 to 8191
- cotangent: bfloat16 [2048, 1024], P(('dp', 'row'), 'col'), may hold values from -6 to 6
Outputs:
- result: bfloat16 [2048, 1024], P(('dp', 'row'), 'col')
- d_input: float32 [2048, 1024], P(('dp', 'row'), 'col')
- g_norm1: float32 [1024], replicated
- g_query: float32 [1024, 1024], P('col', ('row', 'dp'))
- g_key: float32 [1024, 512], P('col', ('row', 'dp'))
- g_value: float32 [1024, 512], P('col', ('row', 'dp'))
- g_qgain: float32 [64], replicated
- g_kgain: float32 [64], replicated
- g_out: float32 [1024, 1024], P('row', ('col', 'dp'))
- g_norm2: float32 [1024], replicated
- g_gate: float32 [1024, 4608], P('col', ('row', 'dp'))
- g_up: float32 [1024, 4608], P('col', ('row', 'dp'))
- g_down: float32 [4608, 1024], P('row', ('col', 'dp'))
The draws below stay inside these ranges and needn't reach their ends.
Inputs may be any that keep to these rules, and one draw needn't show every extreme that they name: `segments`: segment numbers never fall along the tokens; one document spans at most 1024 tokens and may cross sequence ends.
All inputs are finite; a program needn't handle non-finite values.
Results may differ from the reference program's by a relative error of at most 0.018.
Values may be sent and summed in bfloat16 or wider, within the bound.
No kernel may reach another device: no remote copies, remote signals or barrier semaphores. Data moves between devices by JAX's collectives and lax.ppermute only.
A program may use at most 128 MiB of HBM per device.

```python
import math
import jax
import jax.numpy as jnp
import numpy as np
from jax import lax

MODEL_WIDTH = 1024
QUERY_HEADS = 16
KEYVALUE_HEADS = 8
HEAD_SIZE = 64
FEEDFWD_UNITS = 4608
SEQUENCE_TOKENS = 512
QBLK = 512
TOKENS = 2048


def place_ends(values, rng, low, top_value):
    longest = values.shape.index(max(values.shape))
    spots = []
    for shift in (0, 1):
        where = [jax.random.randint(jax.random.fold_in(rng, axis), (), 0, length) for axis, length in enumerate(values.shape)]
        where[longest] = (where[longest] + shift) % values.shape[longest]
        spots.append(tuple(where))
    return values.at[spots[0]].set(low).at[spots[1]].set(top_value)


def block_levels(own_key, dims, split, least, top_value):
    loudness = 1.0
    for position, blocks in split:
        heights = jax.random.uniform(jax.random.fold_in(jax.random.fold_in(own_key, 6), position), (blocks,), jnp.float32, least / len(split), top_value / len(split))
        loudness = loudness * jnp.repeat(jnp.exp(heights), dims[position] // blocks).reshape((-1,) + (1,) * (len(dims) - 1 - position))
    return loudness


def profile(number_of, total, limit, slope):
    portions = [(1 << 20) // math.isqrt(rank ** slope) + 1 for rank in range(2, number_of + 1)]
    rest, given = total - limit - (number_of - 1), [1] * (number_of - 1)
    while rest > 0:
        free = [i for i in range(number_of - 1) if given[i] < limit]
        mass, budget = sum([portions[i] for i in free]), rest
        for i in free:
            more = min(limit - given[i], max(1, budget * portions[i] // mass), rest)
            given[i] = given[i] + more
            rest = rest - more
    return np.array([limit] + given)


def uneven_parts(stream_key, number_of, total, most, lean):
    if number_of == 2:
        one = jax.random.randint(stream_key, (), max(1, total - most), min(most, total - 1) + 1)
        return jnp.stack([one, total - one])
    lengths = jnp.asarray(profile(number_of, total, most, lean), jnp.int32)
    twos = (number_of - 1) // 2
    giver, receiver = lengths[1:1 + 2 * twos:2], lengths[2:2 + 2 * twos:2]
    margin = jnp.minimum(giver - 1, most - receiver)
    passed = jax.random.randint(jax.random.fold_in(stream_key, 1), (twos,), 0, 1 << 20) % (margin + 1)
    lengths = lengths.at[1:1 + 2 * twos:2].set(giver - passed).at[2:2 + 2 * twos:2].set(receiver + passed)
    return lengths[jax.random.permutation(jax.random.fold_in(stream_key, 2), number_of)]


def bell_draw(rng, dims, scale, bound, cuts=(), kind=jnp.bfloat16):
    loudness = block_levels(rng, dims, cuts, -0.22, 0.18) if cuts else 1.0
    values = jax.random.normal(rng, dims, jnp.float32) * scale * loudness
    return jnp.minimum(jnp.maximum(values, -bound), bound).astype(kind)


def setup_inputs(seed: int = 0) -> dict:
    streams_of = jax.random.split(jax.random.key(seed), 16)
    return {
        "block_input": bell_draw(streams_of[0], (TOKENS, MODEL_WIDTH), 1.0, 6.0, ((0, 8), (1, 4))),
        "norm1_gain": jnp.clip(1.0 + 0.18 * jax.random.normal(streams_of[1], (MODEL_WIDTH,), jnp.float32), 0.1, 1.9),
        "query_weight": bell_draw(streams_of[2], (MODEL_WIDTH, QUERY_HEADS * HEAD_SIZE), MODEL_WIDTH ** -0.5, 0.1875, ((0, 4), (1, 2))),
        "key_weight": bell_draw(streams_of[3], (MODEL_WIDTH, KEYVALUE_HEADS * HEAD_SIZE), MODEL_WIDTH ** -0.5, 0.1875, ((0, 4), (1, 2))),
        "value_weight": bell_draw(streams_of[4], (MODEL_WIDTH, KEYVALUE_HEADS * HEAD_SIZE), MODEL_WIDTH ** -0.5, 0.1875, ((0, 4), (1, 2))),
        "query_gain": jnp.clip(1.0 + 0.18 * jax.random.normal(streams_of[5], (HEAD_SIZE,), jnp.float32), 0.1, 1.9),
        "key_gain": jnp.clip(1.0 + 0.18 * jax.random.normal(streams_of[6], (HEAD_SIZE,), jnp.float32), 0.1, 1.9),
        "output_weight": bell_draw(streams_of[7], (QUERY_HEADS * HEAD_SIZE, MODEL_WIDTH), (QUERY_HEADS * HEAD_SIZE // 16) ** -0.5, 0.75, ((0, 2), (1, 4))),
        "norm2_gain": jnp.clip(1.0 + 0.18 * jax.random.normal(streams_of[8], (MODEL_WIDTH,), jnp.float32), 0.1, 1.9),
        "w_gate": bell_draw(streams_of[9], (MODEL_WIDTH, FEEDFWD_UNITS), MODEL_WIDTH ** -0.5, 0.1875, ((0, 4), (1, 2))),
        "w_up": bell_draw(streams_of[10], (MODEL_WIDTH, FEEDFWD_UNITS), MODEL_WIDTH ** -0.5, 0.1875, ((0, 4), (1, 2))),
        "w_down": bell_draw(streams_of[11], (FEEDFWD_UNITS, MODEL_WIDTH), FEEDFWD_UNITS ** -0.5, 0.09375, ((0, 2), (1, 4))),
        "segments": jnp.searchsorted(jnp.cumsum(uneven_parts(streams_of[12], TOKENS * 5 // (3 * SEQUENCE_TOKENS), TOKENS, 2 * SEQUENCE_TOKENS, 0)), jnp.arange(TOKENS), side="right").astype(jnp.int32),
        "positions": place_ends(jax.random.randint(streams_of[13], (TOKENS,), 0, 8192), jax.random.fold_in(streams_of[13], 1), 0, 8191).astype(jnp.int32),
        "cotangent": bell_draw(streams_of[14], (TOKENS, MODEL_WIDTH), 1.0, 6.0, ((0, 8), (1, 4))),
    }


EPS = 1e-05
THETA = 1000000.0

def widen(array):
    return lax.optimization_barrier(array).astype(jnp.float32)

def rope_tables(places):
    half = HEAD_SIZE // 2
    freqs = THETA ** (-(jnp.arange(half, dtype=jnp.float32) * 2.0) / HEAD_SIZE)
    angles = places.astype(jnp.float32)[:, None] * freqs[None, :]
    cosine = jnp.cos(angles)
    sine = jnp.sin(angles)
    return (jnp.concatenate([cosine, cosine], -1), jnp.concatenate([sine, sine], -1))

def rotate_forward(array):
    half = array.shape[-1] // 2
    return jnp.concatenate([-array[..., half:], array[..., :half]], -1)

def rotate_backward(array):
    half = array.shape[-1] // 2
    return jnp.concatenate([array[..., half:], -array[..., :half]], -1)

def block_mask(seg_seq, start, finish):
    query_pos = start + jnp.arange(QBLK)
    key_pos = jnp.arange(finish)
    same = seg_seq[start:finish][:, None] == seg_seq[None, :finish]
    return same & (key_pos[None, :] <= query_pos[:, None])

def attend_forward(query_b, key_b, value_block, seg_seq):
    scale = HEAD_SIZE ** (-0.5)
    query_f = widen(query_b)
    key_f = widen(key_b)
    value_f = widen(value_block)
    outputs = []
    totals = []
    for block_number in range(SEQUENCE_TOKENS // QBLK):
        start = block_number * QBLK
        finish = start + QBLK
        scores = jnp.einsum('qkgd,skd->kgqs', query_f[start:finish], key_f[:finish]) * scale
        scores = jnp.where(block_mask(seg_seq, start, finish), scores, -jnp.inf)
        peak = lax.optimization_barrier(jnp.max(scores, -1, keepdims=True))
        total = jnp.log(lax.optimization_barrier(jnp.sum(jnp.exp(scores - peak), -1, keepdims=True))) + peak
        weights = widen(jnp.exp(scores - total).astype(jnp.bfloat16))
        outputs.append(jnp.einsum('kgqs,skd->qkgd', weights, value_f[:finish]).astype(jnp.bfloat16))
        totals.append(total)
    return (jnp.concatenate(outputs, 0), jnp.concatenate(totals, 2))

def attend_backward(query_b, key_b, value_block, dout_b, delta, totals, seg_seq):
    scale = HEAD_SIZE ** (-0.5)
    query_f = widen(query_b)
    key_f = widen(key_b)
    value_f = widen(value_block)
    dout_f = widen(dout_b)
    dq_parts = []
    dk_sum = jnp.zeros(key_b.shape, jnp.float32)
    dv_sum = jnp.zeros(value_block.shape, jnp.float32)
    for block_number in range(SEQUENCE_TOKENS // QBLK):
        start = block_number * QBLK
        finish = start + QBLK
        scores = jnp.einsum('qkgd,skd->kgqs', query_f[start:finish], key_f[:finish]) * scale
        scores = jnp.where(block_mask(seg_seq, start, finish), scores, -jnp.inf)
        probs = jnp.exp(scores - totals[:, :, start:finish])
        probs_w = widen(probs.astype(jnp.bfloat16))
        d_probs = jnp.einsum('qkgd,skd->kgqs', dout_f[start:finish], value_f[:finish])
        d_scores = probs * (d_probs - jnp.transpose(delta[start:finish], (1, 2, 0))[..., None])
        ds_w = widen(d_scores.astype(jnp.bfloat16))
        dv_sum = dv_sum.at[:finish].add(jnp.einsum('kgqs,qkgd->skd', probs_w, dout_f[start:finish]))
        dq_parts.append(jnp.einsum('kgqs,skd->qkgd', ds_w, key_f[:finish]) * scale)
        dk_sum = dk_sum.at[:finish].add(jnp.einsum('kgqs,qkgd->skd', ds_w, query_f[start:finish]) * scale)
    return (jnp.concatenate(dq_parts, 0), dk_sum, dv_sum)

def float_product(left, right):
    return jnp.dot(left, right, preferred_element_type=jnp.float32)

def reference(block_input, norm1_gain, query_weight, key_weight, value_weight, query_gain, key_gain, output_weight, norm2_gain, w_gate, w_up, w_down, segments, positions, cotangent):
    query_group = QUERY_HEADS // KEYVALUE_HEADS
    count = TOKENS // SEQUENCE_TOKENS

    def one_sequence(carry, pieces):
        x_seq, seg_seq, pos_seq, cot_seq = pieces
        xf = x_seq.astype(jnp.float32)
        inv1 = lax.rsqrt(lax.optimization_barrier(jnp.mean(xf * xf, -1, keepdims=True)) + EPS)
        normalized_input = (xf * inv1 * norm1_gain).astype(jnp.bfloat16)
        query_rows = float_product(normalized_input, query_weight).reshape(SEQUENCE_TOKENS, KEYVALUE_HEADS, query_group, HEAD_SIZE)
        key = float_product(normalized_input, key_weight).reshape(SEQUENCE_TOKENS, KEYVALUE_HEADS, HEAD_SIZE)
        value_block = float_product(normalized_input, value_weight).astype(jnp.bfloat16).reshape(SEQUENCE_TOKENS, KEYVALUE_HEADS, HEAD_SIZE)
        q_scale = lax.rsqrt(lax.optimization_barrier(jnp.mean(query_rows * query_rows, -1, keepdims=True)) + EPS)
        k_scale = lax.rsqrt(lax.optimization_barrier(jnp.mean(key * key, -1, keepdims=True)) + EPS)
        q_norm = query_rows * q_scale * query_gain
        k_norm = key * k_scale * key_gain
        cosine, sine = rope_tables(pos_seq)
        query_b = (q_norm * cosine[:, None, None, :] + rotate_forward(q_norm) * sine[:, None, None, :]).astype(jnp.bfloat16)
        key_b = (k_norm * cosine[:, None, :] + rotate_forward(k_norm) * sine[:, None, :]).astype(jnp.bfloat16)
        attended, totals = attend_forward(query_b, key_b, value_block, seg_seq)
        att_flat = attended.reshape(SEQUENCE_TOKENS, QUERY_HEADS * HEAD_SIZE)
        mixed = xf + float_product(att_flat, output_weight)
        inv2 = lax.rsqrt(lax.optimization_barrier(jnp.mean(mixed * mixed, -1, keepdims=True)) + EPS)
        normed2 = (mixed * inv2 * norm2_gain).astype(jnp.bfloat16)
        gate = float_product(normed2, w_gate)
        up_val = float_product(normed2, w_up)
        sig = jax.nn.sigmoid(gate)
        hidden = (gate * sig * up_val).astype(jnp.bfloat16)
        out_seq = (mixed + float_product(hidden, w_down)).astype(jnp.bfloat16)
        d_hidden = float_product(cot_seq, w_down.T)
        grad_down = float_product(hidden.T, cot_seq)
        d_gate = (d_hidden * up_val * sig * (1.0 + gate * (1.0 - sig))).astype(jnp.bfloat16)
        d_up = (d_hidden * gate * sig).astype(jnp.bfloat16)
        d_normed2 = float_product(d_gate, w_gate.T) + float_product(d_up, w_up.T)
        grad_gate = float_product(normed2.T, d_gate)
        grad_up = float_product(normed2.T, d_up)
        scaled2 = d_normed2 * norm2_gain
        gain2 = lax.optimization_barrier(jnp.sum(d_normed2 * mixed * inv2, 0))
        d_mixed = cot_seq.astype(jnp.float32) + inv2 * scaled2 - mixed * (inv2 * inv2 * inv2) * lax.optimization_barrier(jnp.mean(scaled2 * mixed, -1, keepdims=True))
        mixed_gradient_block = d_mixed.astype(jnp.bfloat16)
        grad_out = float_product(att_flat.T, mixed_gradient_block)
        attention_gradient = float_product(mixed_gradient_block, output_weight.T).reshape(SEQUENCE_TOKENS, KEYVALUE_HEADS, query_group, HEAD_SIZE)
        delta = lax.optimization_barrier(jnp.sum(attention_gradient * attended.astype(jnp.float32), -1))
        d_att_b = attention_gradient.astype(jnp.bfloat16)
        dq_rot, dk_rot, value_gradient = attend_backward(query_b, key_b, value_block, d_att_b, delta, totals, seg_seq)
        dq_norm = dq_rot * cosine[:, None, None, :] + rotate_backward(dq_rot * sine[:, None, None, :])
        dk_norm = dk_rot * cosine[:, None, :] + rotate_backward(dk_rot * sine[:, None, :])
        qgain = lax.optimization_barrier(jnp.sum(dq_norm * query_rows * q_scale, (0, 1, 2)))
        kgain = lax.optimization_barrier(jnp.sum(dk_norm * key * k_scale, (0, 1)))
        scaled_q = dq_norm * query_gain
        scaled_k = dk_norm * key_gain
        d_query = q_scale * scaled_q - query_rows * (q_scale * q_scale * q_scale) * lax.optimization_barrier(jnp.mean(scaled_q * query_rows, -1, keepdims=True))
        key_gradient = k_scale * scaled_k - key * (k_scale * k_scale * k_scale) * lax.optimization_barrier(jnp.mean(scaled_k * key, -1, keepdims=True))
        dq_b = d_query.reshape(SEQUENCE_TOKENS, QUERY_HEADS * HEAD_SIZE).astype(jnp.bfloat16)
        key_gradient_block = key_gradient.reshape(SEQUENCE_TOKENS, KEYVALUE_HEADS * HEAD_SIZE).astype(jnp.bfloat16)
        value_gradient_block = value_gradient.reshape(SEQUENCE_TOKENS, KEYVALUE_HEADS * HEAD_SIZE).astype(jnp.bfloat16)
        d_normed = float_product(dq_b, query_weight.T) + float_product(key_gradient_block, key_weight.T) + float_product(value_gradient_block, value_weight.T)
        grad_query = float_product(normalized_input.T, dq_b)
        grad_key = float_product(normalized_input.T, key_gradient_block)
        grad_value = float_product(normalized_input.T, value_gradient_block)
        scaled1 = d_normed * norm1_gain
        gain1 = lax.optimization_barrier(jnp.sum(d_normed * xf * inv1, 0))
        d_in = d_mixed + inv1 * scaled1 - xf * (inv1 * inv1 * inv1) * lax.optimization_barrier(jnp.mean(scaled1 * xf, -1, keepdims=True))
        terms = (gain1, grad_query, grad_key, grad_value, qgain, kgain, grad_out, gain2, grad_gate, grad_up, grad_down)
        carry = tuple((total + term for total, term in zip(carry, terms)))
        return (carry, (out_seq, d_in))
    zero_filled = (jnp.zeros((MODEL_WIDTH,), jnp.float32), jnp.zeros((MODEL_WIDTH, QUERY_HEADS * HEAD_SIZE), jnp.float32), jnp.zeros((MODEL_WIDTH, KEYVALUE_HEADS * HEAD_SIZE), jnp.float32), jnp.zeros((MODEL_WIDTH, KEYVALUE_HEADS * HEAD_SIZE), jnp.float32), jnp.zeros((HEAD_SIZE,), jnp.float32), jnp.zeros((HEAD_SIZE,), jnp.float32), jnp.zeros((QUERY_HEADS * HEAD_SIZE, MODEL_WIDTH), jnp.float32), jnp.zeros((MODEL_WIDTH,), jnp.float32), jnp.zeros((MODEL_WIDTH, FEEDFWD_UNITS), jnp.float32), jnp.zeros((MODEL_WIDTH, FEEDFWD_UNITS), jnp.float32), jnp.zeros((FEEDFWD_UNITS, MODEL_WIDTH), jnp.float32))
    inputs = (block_input.reshape(count, SEQUENCE_TOKENS, MODEL_WIDTH), segments.reshape(count, SEQUENCE_TOKENS), positions.reshape(count, SEQUENCE_TOKENS), cotangent.reshape(count, SEQUENCE_TOKENS, MODEL_WIDTH))
    sums, (outs, d_ins) = lax.scan(one_sequence, zero_filled, inputs)
    return (outs.reshape(TOKENS, MODEL_WIDTH), d_ins.reshape(TOKENS, MODEL_WIDTH), sums[0], sums[1], sums[2], sums[3], sums[4], sums[5], sums[6], sums[7], sums[8], sums[9], sums[10])
```

```python
import jax
import jax.numpy as jnp
from jax import lax
from jax.sharding import PartitionSpec as P

QUERY_HEADS = 16
KEYVALUE_HEADS = 8
HEAD_SIZE = 64
SEQUENCE_TOKENS = 512

EPS = 1e-05
THETA = 1000000.0
WIDE = 8


F32 = jnp.float32
BF16 = jnp.bfloat16


def swap(x, axis, k):
    n = lax.axis_size(axis)
    return lax.ppermute(x, axis, [(i, i ^ k) for i in range(n)])


def exchange(blocks, axis):
    return [blocks[0]] + [swap(b, axis, k) for k, b in enumerate(blocks) if k]


def gather_rel(x, axis):
    return exchange([x] * lax.axis_size(axis), axis)


def dp_gather(x):
    n = lax.axis_size("dp")
    if n > WIDE:
        return lax.all_gather(x, "dp")
    me = lax.axis_index("dp")
    out = jnp.zeros((n,) + x.shape, x.dtype)
    for k, part in enumerate(gather_rel(x, "dp")):
        out = lax.dynamic_update_index_in_dim(out, part, me ^ k, 0)
    return out


def dp_scatter(pieces):
    n = lax.axis_size("dp")
    if n > WIDE:
        stack = jnp.stack([pieces(j) for j in range(n)])
        return lax.psum_scatter(stack, "dp", scatter_dimension=0, tiled=False).astype(F32)
    me = lax.axis_index("dp")
    got = exchange([pieces(me ^ k) for k in range(n)], "dp")
    return sum(g.astype(F32) for g in got)


def all_sum(x, axis):
    n = lax.axis_size(axis)
    if n > WIDE:
        return lax.psum(x, axis)
    parts = gather_rel(x, axis)
    while len(parts) > 1:
        parts = [parts[i] + parts[i + 1] for i in range(0, len(parts), 2)]
    return parts[0]


def split_high(x):
    high = lax.reduce_precision(x, 8, 7)
    return high.astype(BF16), (x - high).astype(BF16)


def nn(a, b):
    return jnp.dot(a, b, preferred_element_type=F32)


def nt(a, b):
    return lax.dot_general(a, b, (((1,), (1,)), ((), ())), preferred_element_type=F32)


def tn(a, b):
    return lax.dot_general(a, b, (((0,), (0,)), ((), ())), preferred_element_type=F32)


def rope_tables(places):
    half = HEAD_SIZE // 2
    freqs = THETA ** (-(jnp.arange(half, dtype=F32) * 2.0) / HEAD_SIZE)
    angles = places.astype(F32)[:, None] * freqs[None, :]
    cosine = jnp.cos(angles)
    sine = jnp.sin(angles)
    return (jnp.concatenate([cosine, cosine], -1), jnp.concatenate([sine, sine], -1))


def rotate_forward(array):
    half = array.shape[-1] // 2
    return jnp.concatenate([-array[..., half:], array[..., :half]], -1)


def rotate_backward(array):
    half = array.shape[-1] // 2
    return jnp.concatenate([array[..., half:], -array[..., :half]], -1)


def rows_of(vec, width):
    high, low = split_high(vec)
    block = jnp.concatenate([high.reshape(-1, width), low.reshape(-1, width)], 0)
    return jnp.pad(block, ((0, 16 - block.shape[0]), (0, 0)))


def vec_of(block, count):
    n = count // block.shape[1]
    return (block[:n].astype(F32) + block[n : 2 * n].astype(F32)).reshape(count)


def local(
    block_input,
    norm1_gain,
    query_weight,
    key_weight,
    value_weight,
    query_gain,
    key_gain,
    output_weight,
    norm2_gain,
    w_gate,
    w_up,
    w_down,
    segments,
    positions,
    cotangent,
):
    rows, cols, dps = (lax.axis_size(a) for a in ("row", "col", "dp"))
    ri, ci, di = (lax.axis_index(a) for a in ("row", "col", "dp"))
    own, part = block_input.shape
    tokens = segments.shape[0]
    width = part * cols
    group = QUERY_HEADS // KEYVALUE_HEADS

    def cut(array, index, size, axis):
        return lax.dynamic_slice_in_dim(array, index * size, size, axis)

    def other_tokens(array):
        return jnp.concatenate([array[own:], array[:own]], 0)

    def gather_tokens(blocks):
        mine = jnp.concatenate(blocks, 1)
        return jnp.concatenate([mine, swap(mine, "row", 1)], 0)

    g1h, g1l = split_high(norm1_gain)
    g2h, g2l = split_high(norm2_gain)
    gain_rows = jnp.pad(jnp.stack([g1h, g1l, g2h, g2l]), ((0, 12), (0, 0)))
    got = gather_rel(jnp.concatenate([block_input, gain_rows], 0), "col")
    x_all = gather_tokens([g[:own] for g in got])
    gains = jnp.concatenate([g[own : own + 4] for g in got], 1).astype(F32)
    gain1 = gains[0] + gains[1]
    gain2 = gains[2] + gains[3]

    hq = query_weight.shape[1] // cols
    hk = key_weight.shape[1] // cols
    wqkv = jnp.concatenate(
        exchange(
            [
                jnp.concatenate(
                    [
                        cut(query_weight, ci ^ k, hq, 1),
                        cut(key_weight, ci ^ k, hk, 1),
                        cut(value_weight, ci ^ k, hk, 1),
                    ],
                    1,
                )
                for k in range(cols)
            ],
            "col",
        ),
        0,
    )

    wo_piece = cut(output_weight, di, output_weight.shape[0] // dps, 0)
    wo_rows = dp_gather(jnp.concatenate(gather_rel(wo_piece, "col"), 1)).reshape(cols, -1, width)
    wo_mine = jnp.concatenate(
        [lax.dynamic_index_in_dim(wo_rows, ci ^ k, 0, False) for k in range(cols)], 0
    )
    wo = jnp.concatenate([wo_mine, swap(wo_mine, "row", 1)], 0)

    fd = w_gate.shape[1] // dps
    fs = fd // cols
    ff_cut = [cut(w_gate, di, fd, 1).T, cut(w_up, di, fd, 1).T, cut(w_down, di, fd, 0)]
    ff_sent = [jnp.stack([cut(w, ci ^ k, fs, 0) for w in ff_cut]) for k in range(cols)]
    ff_piece = jnp.concatenate(exchange(ff_sent, "col"), 2)
    ff_all = dp_gather(ff_piece)
    wg, wu, wd = (ff_all[:, i].reshape(dps * fs, width) for i in range(3))

    cot_all = gather_tokens(gather_rel(cotangent, "col"))

    xf = x_all.astype(F32)
    inv1 = lax.rsqrt(jnp.mean(xf * xf, -1, keepdims=True) + EPS)
    xn = (xf * inv1 * gain1).astype(BF16)
    qkv = nn(xn, wqkv)
    kv = hk // HEAD_SIZE
    q = qkv[:, :hq].reshape(tokens, kv, group, HEAD_SIZE)
    k = qkv[:, hq : hq + hk].reshape(tokens, kv, HEAD_SIZE)
    vb = qkv[:, hq + hk :].astype(BF16).reshape(tokens, kv, HEAD_SIZE)
    rq = lax.rsqrt(jnp.mean(q * q, -1, keepdims=True) + EPS)
    rk = lax.rsqrt(jnp.mean(k * k, -1, keepdims=True) + EPS)
    qn = q * rq * query_gain
    kn = k * rk * key_gain

    def relative(vec):
        return jnp.concatenate([cut(vec, ri ^ j, own, 0) for j in range(rows)], 0)

    place = relative(jnp.arange(tokens, dtype=jnp.int32))
    segs = relative(segments)
    cosine, sine = rope_tables(relative(positions))
    cq, sq = cosine[:, None, None, :], sine[:, None, None, :]
    ck, sk = cosine[:, None, :], sine[:, None, :]
    qb = (qn * cq + rotate_forward(qn) * sq).astype(BF16)
    kb = (kn * ck + rotate_forward(kn) * sk).astype(BF16)
    allowed = (
        (segs[:, None] == segs[None, :])
        & (place[None, :] <= place[:, None])
        & (place[None, :] // SEQUENCE_TOKENS == place[:, None] // SEQUENCE_TOKENS)
    )
    scale = HEAD_SIZE ** (-0.5)
    score = jnp.einsum("qkgd,skd->kgqs", qb, kb, preferred_element_type=F32) * scale
    score = jnp.where(allowed, score, -jnp.inf)
    peak = jnp.max(score, -1, keepdims=True)
    lse = jnp.log(jnp.sum(jnp.exp(score - peak), -1, keepdims=True)) + peak
    prob = jnp.exp(score - lse)
    pb = prob.astype(BF16)
    ob = jnp.einsum("kgqs,skd->qkgd", pb, vb, preferred_element_type=F32).astype(BF16)
    ob = ob.reshape(tokens, hq)

    ob_cols = jnp.concatenate(gather_rel(ob, "col"), 1)
    ob_all = jnp.concatenate([ob_cols, other_tokens(swap(ob_cols, "row", 1))], 1)
    h1 = xf + nn(ob_all, wo)
    inv2 = lax.rsqrt(jnp.mean(h1 * h1, -1, keepdims=True) + EPS)
    hn = (h1 * inv2 * gain2).astype(BF16)

    gate = nt(hn, wg)
    up = nt(hn, wu)
    sg = jax.nn.sigmoid(gate)
    hid = (gate * sg * up).astype(BF16)
    dhid = nt(cot_all, wd)
    dgb = (dhid * up * sg * (1.0 + gate * (1.0 - sg))).astype(BF16)
    dub = (dhid * gate * sg).astype(BF16)

    def to_owners(partial, sums):
        mine, far = partial[:own].astype(BF16), partial[own:].astype(BF16)
        if sums is None:
            both = mine.astype(F32) + swap(far, "row", 1).astype(F32)
            blocks = [both[:, j * part : (j + 1) * part].astype(BF16) for j in range(cols)]
            return sum(b.astype(F32) for b in exchange(blocks, "col")), None
        far = jnp.concatenate(
            [far, jnp.pad(rows_of(sums[own:], part), ((0, 0), (0, width - part)))], 0
        )
        came = swap(far, "row", 1)
        both = partial[:own] + came[:own].astype(F32)
        total = rows_of(sums[:own] + vec_of(came[own:, :part], own), part)
        blocks = [
            jnp.concatenate([both[:, j * part : (j + 1) * part].astype(BF16), total], 0)
            for j in range(cols)
        ]
        back = exchange(blocks, "col")
        return (
            sum(b[:own].astype(F32) for b in back),
            sum(vec_of(b[own:], own) for b in back),
        )

    dhn_part = nn(dgb, wg) + nn(dub, wu)
    u2h = jnp.sum(dhn_part * gain2 * h1, -1)
    g2_part = jnp.sum(dhn_part * h1 * inv2, 0)
    dhn, u2h = to_owners(dhn_part, u2h)
    h1_own, inv2_own = h1[:own, :part], inv2[:own]
    dh1 = (
        cotangent.astype(F32)
        + inv2_own * (dhn * norm2_gain)
        - h1_own * (inv2_own * inv2_own * inv2_own) * (u2h[:, None] / width)
    )
    dh1_all = gather_tokens(gather_rel(dh1.astype(BF16), "col"))

    result = (h1_own + to_owners(nn(hid, wd), None)[0]).astype(BF16)

    def hidden_grad(d):
        full = tn(d, hn).astype(BF16)
        mine = dp_scatter(lambda j: cut(full, j, fs, 0)).astype(BF16)
        back = exchange([mine[:, j * part : (j + 1) * part] for j in range(cols)], "col")
        out = jnp.zeros((cols, fs, part), BF16)
        for j, b in enumerate(back):
            out = lax.dynamic_update_index_in_dim(out, b, ci ^ j, 0)
        return out.reshape(fd, part).T.astype(F32)

    def feature_grad(left, right):
        full = tn(left, right).astype(BF16).reshape(cols, dps, part // dps, right.shape[1])
        mine = dp_scatter(
            lambda j: lax.dynamic_index_in_dim(full, j, 1, False)
        ).astype(BF16)
        back = exchange([mine[j] for j in range(cols)], "col")
        out = jnp.zeros((cols,) + back[0].shape, BF16)
        for j, b in enumerate(back):
            out = lax.dynamic_update_index_in_dim(out, b, ci ^ j, 0)
        return out.astype(F32).transpose(0, 2, 1)

    g_down = feature_grad(cot_all, hid)
    g_down = g_down.reshape(cols, dps, fs, -1).transpose(1, 0, 2, 3).reshape(-1, part // dps)
    g_gate = hidden_grad(dgb)
    g_up = hidden_grad(dub)

    do = nt(dh1_all, wo_mine[:hq])
    delta = jnp.sum((do * ob.astype(F32)).reshape(tokens, kv, group, HEAD_SIZE), -1)
    dob = do.astype(BF16).reshape(tokens, kv, group, HEAD_SIZE)
    dp = jnp.einsum("qkgd,skd->kgqs", dob, vb, preferred_element_type=F32)
    dsb = (prob * (dp - jnp.transpose(delta, (1, 2, 0))[..., None])).astype(BF16)
    dv = jnp.einsum("kgqs,qkgd->skd", pb, dob, preferred_element_type=F32)
    dqr = jnp.einsum("kgqs,skd->qkgd", dsb, kb, preferred_element_type=F32) * scale
    dkr = jnp.einsum("kgqs,qkgd->skd", dsb, qb, preferred_element_type=F32) * scale
    dqn = dqr * cq + rotate_backward(dqr * sq)
    dkn = dkr * ck + rotate_backward(dkr * sk)
    qg_part = jnp.sum(dqn * q * rq, (0, 1, 2))
    kg_part = jnp.sum(dkn * k * rk, (0, 1))
    uq = dqn * query_gain
    uk = dkn * key_gain
    dq = rq * uq - q * (rq * rq * rq) * jnp.mean(uq * q, -1, keepdims=True)
    dk = rk * uk - k * (rk * rk * rk) * jnp.mean(uk * k, -1, keepdims=True)
    dqkv = jnp.concatenate(
        [dq.reshape(tokens, hq), dk.reshape(tokens, hk), dv.reshape(tokens, hk)], 1
    ).astype(BF16)

    dxn_part = nt(dqkv, wqkv)
    u1x = jnp.sum(dxn_part * gain1 * xf, -1)
    g1_part = jnp.sum(dxn_part * xf * inv1, 0)
    dxn, u1x = to_owners(dxn_part, u1x)
    inv1_own = inv1[:own]
    d_input = (
        dh1
        + inv1_own * (dxn * norm1_gain)
        - block_input.astype(F32) * (inv1_own * inv1_own * inv1_own) * (u1x[:, None] / width)
    )

    g_out = feature_grad(dh1_all, ob).reshape(cols * hq, part // dps)

    m = dps // cols
    full = tn(xn, dqkv).astype(BF16)

    def qkv_piece(j):
        block = cut(full, (j // m) ^ ci, part, 0)
        return jnp.concatenate(
            [
                cut(block[:, :hq], j % m, hq // m, 1),
                cut(block[:, hq : hq + hk], j % m, hk // m, 1),
                cut(block[:, hq + hk :], j % m, hk // m, 1),
            ],
            1,
        )

    g_qkv = lax.ppermute(
        dp_scatter(qkv_piece).astype(BF16),
        ("dp", "col"),
        [
            (p * cols + c, (c * m + p % m) * cols + p // m)
            for p in range(dps)
            for c in range(cols)
        ],
    ).astype(F32)
    g_query = g_qkv[:, : hq // m]
    g_key = g_qkv[:, hq // m : (hq + hk) // m]
    g_value = g_qkv[:, (hq + hk) // m :]

    def in_order(vec):
        return jnp.concatenate([cut(vec, ci ^ j, part, 0) for j in range(cols)], 0)

    vec = jnp.concatenate([in_order(g1_part), in_order(g2_part), qg_part, kg_part])
    for axis in ("row", "col", "dp"):
        vec = all_sum(vec, axis)
    g_norm1 = vec[:width]
    g_norm2 = vec[width : 2 * width]
    g_qgain = vec[2 * width : 2 * width + HEAD_SIZE]
    g_kgain = vec[2 * width + HEAD_SIZE :]
    return (
        result,
        d_input,
        g_norm1,
        g_query,
        g_key,
        g_value,
        g_qgain,
        g_kgain,
        g_out,
        g_norm2,
        g_gate,
        g_up,
        g_down,
    )


def solution(mesh):
    in_specs = (
        P(("dp", "row"), "col"),
        P("col"),
        P("col", "row"),
        P("col", "row"),
        P("col", "row"),
        P(),
        P(),
        P("row", "col"),
        P("col"),
        P("col", "row"),
        P("col", "row"),
        P("row", "col"),
        P("dp"),
        P("dp"),
        P(("dp", "row"), "col"),
    )
    out_specs = (
        P(("dp", "row"), "col"),
        P(("dp", "row"), "col"),
        P(),
        P("col", ("row", "dp")),
        P("col", ("row", "dp")),
        P("col", ("row", "dp")),
        P(),
        P(),
        P("row", ("col", "dp")),
        P(),
        P("col", ("row", "dp")),
        P("col", ("row", "dp")),
        P("row", ("col", "dp")),
    )
    return jax.shard_map(local, mesh=mesh, in_specs=in_specs, out_specs=out_specs, check_vma=False)
```

```python
import jax
import jax.numpy as jnp
from jax import lax
from jax.experimental import pallas as pl
from jax.experimental.pallas import tpu as pltpu
from jax.sharding import PartitionSpec as P


QUERY_HEADS = 16
KEYVALUE_HEADS = 8
HEAD_SIZE = 64
SEQUENCE_TOKENS = 512

EPS = 1e-05
THETA = 1000000.0
WIDE = 8


F32 = jnp.float32
BF16 = jnp.bfloat16


def swap(x, axis, k):
    n = lax.axis_size(axis)
    return lax.ppermute(x, axis, [(i, i ^ k) for i in range(n)])


def exchange(blocks, axis):
    return [blocks[0]] + [swap(b, axis, k) for k, b in enumerate(blocks) if k]


def rel_order(n):
    order = [0]
    bit = n // 2
    while bit:
        order += [o ^ bit for o in order]
        bit //= 2
    return order


def gather_cols(x, late=None):
    bit = lax.axis_size("col") // 2
    while bit:
        came = swap(x, "col", bit)
        if late is not None:
            came, late = after(came, late[0]), late[1:]
        x = jnp.concatenate([x, came], 1)
        bit //= 2
    return x


def gather_direct(x):
    cols = lax.axis_size("col")
    got = {o: swap(x, "col", o) for o in range(cols - 1, 0, -1)}
    got[0] = x
    return jnp.concatenate([got[o] for o in rel_order(cols)], 1)


def gather_parts(x, late):
    parts = [x]
    bit = lax.axis_size("col") // 2
    while bit:
        sent = parts[0] if len(parts) == 1 else jnp.concatenate(parts, 1)
        came = swap(sent, "col", bit)
        parts.append(after(came, late) if len(parts) == 1 else came)
        bit //= 2
    return parts


def dp_scatter(pieces, late=None):
    n = lax.axis_size("dp")
    if n > WIDE:
        stack = jnp.stack([pieces(j) for j in range(n)])
        return lax.psum_scatter(stack, "dp", scatter_dimension=0, tiled=False).astype(F32)
    me = lax.axis_index("dp")
    got = exchange([pieces(me ^ k) for k in range(n)], "dp")
    if late is not None:
        got = after(got, late)
    return sum(g.astype(F32) for g in got)


def split_high(x):
    high = lax.reduce_precision(x, 8, 7)
    return high.astype(BF16), (x - high).astype(BF16)


def nn(a, b):
    return jnp.dot(a, b, preferred_element_type=F32)


def nt(a, b):
    return lax.dot_general(a, b, (((1,), (1,)), ((), ())), preferred_element_type=F32)


def tn(a, b):
    return lax.dot_general(a, b, (((0,), (0,)), ((), ())), preferred_element_type=F32)


def rope_tables(places):
    half = HEAD_SIZE // 2
    freqs = THETA ** (-(jnp.arange(half, dtype=F32) * 2.0) / HEAD_SIZE)
    angles = places.astype(F32)[:, None] * freqs[None, :]
    cosine = jnp.cos(angles)
    sine = jnp.sin(angles)
    return (jnp.concatenate([cosine, cosine], -1), jnp.concatenate([sine, sine], -1))


def rotate_forward(array):
    half = array.shape[-1] // 2
    return jnp.concatenate([-array[..., half:], array[..., :half]], -1)


def rotate_backward(array):
    half = array.shape[-1] // 2
    return jnp.concatenate([array[..., half:], -array[..., :half]], -1)


VMEM = pl.BlockSpec(memory_space=pltpu.VMEM)
SMEM = pl.BlockSpec(memory_space=pltpu.SMEM)


def kernel_call(body, outs, ins, scratch=(), scalars=0):
    return pl.pallas_call(
        body,
        out_shape=[jax.ShapeDtypeStruct(shape, dtype) for shape, dtype in outs],
        in_specs=[SMEM] * scalars + [VMEM] * (len(ins) - scalars),
        out_specs=[VMEM] * len(outs),
        scratch_shapes=list(scratch),
        compiler_params=pltpu.CompilerParams(vmem_limit_bytes=56 * 1024 * 1024),
    )(*ins)


def row_sums(array):
    ones = jnp.ones((8, array.shape[1]), BF16)
    high = array.astype(BF16)
    low = (array - high.astype(F32)).astype(BF16)
    return nt(ones, high) + nt(ones, low)


def put_row(ref, start, row):
    n = row.shape[1]
    if ref.shape[1] > n:
        ref[start : start + 16, :] = jnp.zeros((16, ref.shape[1]), BF16)
    high = row.astype(BF16)
    low = (row - high.astype(F32)).astype(BF16)
    ref[start : start + 16, :n] = jnp.concatenate([high.astype(F32), low.astype(F32)], 0).astype(
        BF16
    )


def packed(array, row):
    array = array.astype(BF16)
    if row is None:
        return array
    extra = jnp.concatenate([jnp.broadcast_to(p, (8, p.shape[1])) for p in split_high(row)], 0)
    return jnp.concatenate(
        [array, jnp.pad(extra, ((0, 0), (0, array.shape[1] - extra.shape[1])))], 0
    )


def after(x, late):
    return lax.optimization_barrier((x, late))[0]


def owners(keep, row, msg):
    own, width = keep.shape
    cols = lax.axis_size("col")
    part = width // cols

    def plus(keep, row, came):
        more = None
        if row is not None:
            n = row.shape[1]
            more = row + came[own : own + 1, :n].astype(F32) + came[own + 8 : own + 9, :n].astype(F32)
        return keep + came[:own].astype(F32), more

    keep, row = plus(keep, row, swap(msg, "row", 1))
    sent = {
        o: packed(keep[:, i * part : (i + 1) * part], row)
        for i, o in enumerate(rel_order(cols))
        if o
    }
    came = [swap(sent[o], "col", o) for o in sorted(sent, reverse=True)]
    near = (keep[:, :part], row)

    def finish(late=None):
        got = came if late is None else after(came, late)
        total = near
        for c in got:
            total = plus(*total, c)
        return total

    return finish, tuple(sent.values())


def project(index, obs, own_wo, wo_pieces, wq, whole):
    tokens = obs[0].shape[0]
    heads, part = own_wo.shape
    width = part * (1 + wo_pieces[0].shape[0]) if not whole else part + wo_pieces[0].shape[1]
    blocks = 4
    wc = heads // blocks

    def body(*refs):
        index_ref, own_ref = refs[:2]
        ob_refs = refs[2 : 2 + len(obs)]
        w_refs = refs[2 + len(obs) : 2 + len(obs) + len(wo_pieces)]
        keep_ref, send_ref, w_s = refs[2 + len(obs) + len(wo_pieces) :]
        for k in range(blocks):
            at = pl.ds(pl.multiple_of(index_ref[8 + k], 16), wc)
            w_s[at, :part] = own_ref[k * wc : (k + 1) * wc, :]
        if whole:
            w_s[:, part:] = w_refs[0][...]
        else:
            for k, w in enumerate(w_refs):
                at = pl.ds(pl.multiple_of(index_ref[4 + k], 16), wq)
                for p in range(w.shape[0]):
                    w_s[at, (p + 1) * part : (p + 2) * part] = w[p]
        start = 0
        total = None
        for o in ob_refs:
            n = o.shape[1]
            term = nn(o[...], w_s[start : start + n, :])
            total = term if total is None else total + term
            start += n
        keep_ref[...] = total
        send_ref[...] = total.astype(BF16)

    if whole:
        taken = pl.BlockSpec(wo_pieces[0].shape, lambda i: (0, 0))
    else:
        taken = pl.BlockSpec((wo_pieces[0].shape[0], wq, part), lambda i: (0, 0, 0))
    full = [pl.BlockSpec(o.shape, lambda i: (0, 0)) for o in (own_wo, *obs)]
    return pl.pallas_call(
        body,
        grid=(1,),
        out_shape=[
            jax.ShapeDtypeStruct((tokens, width), F32),
            jax.ShapeDtypeStruct((tokens, width), BF16),
        ],
        in_specs=[SMEM, *full, *[taken] * len(wo_pieces)],
        out_specs=[pl.BlockSpec((tokens, width), lambda i: (0, 0))] * 2,
        scratch_shapes=[pltpu.VMEM((heads, width), BF16)],
        compiler_params=pltpu.CompilerParams(vmem_limit_bytes=56 * 1024 * 1024),
        name="project",
    )(index, own_wo, *obs, *wo_pieces)


def feed_forward(index, x, mixed, mixed_far, mine, pieces, cot, gain, sizes):
    own, fs, part = sizes
    tokens, width = mixed.shape
    whole = len(pieces) == 3
    fd = mine[0].shape[0]

    def body(*refs):
        index_ref, x0, x1, mix_ref, far_ref, c0, c1, gain_ref = refs[:8]
        own_refs = refs[8:11]
        piece_refs = refs[11 : 11 + len(pieces)]
        (dn_keep, dn_row, dn_msg, rs_keep, rs_msg, hid_ref, dgb_ref, dub_ref, hn_ref, h1_ref,
         inv_ref, g2_ref, wg_s, wu_s, wd_s) = refs[11 + len(pieces) :]
        for target, own_w in zip((wg_s, wu_s, wd_s), own_refs):
            target[:, :part] = own_w[...]
        if whole:
            for target, rest in zip((wg_s, wu_s, wd_s), piece_refs):
                target[:, part:] = rest[...]
        else:
            for k in range(4):
                at = pl.ds(pl.multiple_of(index_ref[k], 16), fs)
                gate_up = piece_refs[k]
                skip = gate_up.shape[1] - 2 * fs
                down = piece_refs[k if k < 3 else 4]
                skip_down = skip - fs if k < 3 else down.shape[1] - fs
                for p in range(gate_up.shape[0]):
                    lanes = slice((p + 1) * part, (p + 2) * part)
                    wg_s[at, lanes] = gate_up[p, skip : skip + fs, :]
                    wu_s[at, lanes] = gate_up[p, skip + fs :, :]
                    wd_s[at, lanes] = down[p, skip_down : skip_down + fs, :]
        gain_ = gain_ref[...]
        for step in range(2):
            near = slice(step * own, (step + 1) * own)
            other = slice((1 - step) * own, (2 - step) * own)
            h1 = (x0, x1)[step][...].astype(F32) + mix_ref[near, :] + far_ref[other, :].astype(F32)
            inv = lax.rsqrt(jnp.mean(h1 * h1, -1, keepdims=True) + EPS)
            hn = (h1 * inv * gain_).astype(BF16)
            hn_ref[near, :] = hn
            gate = nt(hn, wg_s[...])
            up = nt(hn, wu_s[...])
            sg = jax.nn.sigmoid(gate)
            act = gate * sg
            hid = (act * up).astype(BF16)
            hid_ref[near, :] = hid
            dhid = nt((c0, c1)[step][...], wd_s[...])
            dgb = (dhid * up * sg * (1.0 + gate * (1.0 - sg))).astype(BF16)
            dub = (dhid * act).astype(BF16)
            dgb_ref[near, :] = dgb
            dub_ref[near, :] = dub
            dhn = nn(dgb, wg_s[...]) + nn(dub, wu_s[...])
            res = nn(hid, wd_s[...])
            dh = dhn * h1
            gsum = jnp.sum(dh * inv, 0, keepdims=True)
            sums = row_sums(dh * gain_)
            if step == 0:
                h1_ref[...] = h1[:, :part]
                inv_ref[...] = inv
                dn_keep[...] = dhn
                rs_keep[...] = res
                dn_row[...] = sums
                g2_ref[...] = gsum
            else:
                dn_msg[:own, :] = dhn.astype(BF16)
                put_row(dn_msg, own, sums)
                rs_msg[...] = res.astype(BF16)
                g2_ref[...] += gsum

    outs = [
        ((own, width), F32),
        ((8, own), F32),
        ((own + 16, width), BF16),
        ((own, width), F32),
        ((own, width), BF16),
        ((tokens, fd), BF16),
        ((tokens, fd), BF16),
        ((tokens, fd), BF16),
        ((tokens, width), BF16),
        ((own, part), F32),
        ((own, 1), F32),
        ((1, width), F32),
    ]
    scratch = [pltpu.VMEM((fd, width), BF16)] * 3
    ins = [index, *x, mixed, mixed_far, *cot, gain, *mine, *pieces]
    return kernel_call(body, outs, ins, scratch, 1)


def gate_up_blocks(index, blocks, fs):
    part = blocks[0].shape[1]
    fd = len(blocks) * fs

    def body(index_ref, *refs):
        srcs, outs, place = refs[: len(blocks)], refs[len(blocks) : -1], refs[-1]
        for i, out in enumerate(outs):
            for j, src in enumerate(srcs):
                at = pl.ds(pl.multiple_of(index_ref[j] * fs, 8), fs)
                place[at, :] = src[...].astype(F32)[i * fs : (i + 1) * fs, :]
            out[...] = place[...]

    return kernel_call(
        body, [((fd, part), F32)] * 2, [index, *blocks], [pltpu.VMEM((fd, part), F32)], 1
    )


def feature_blocks(index, blocks, fs, dps):
    rows, fd = blocks[0].shape
    count = len(blocks)

    def body(index_ref, *refs):
        srcs, (out, stack) = refs[:count], refs[count:]
        for j, src in enumerate(srcs):
            stack[j] = src[...].astype(F32)
        for c in range(count):
            x = stack[index_ref[c]]
            for d in range(dps):
                start = (d * count + c) * fs
                out[:, start : start + fs] = x[:, d * fs : (d + 1) * fs]

    return kernel_call(
        body, [((rows, count * fd), F32)], [index, *blocks], [pltpu.VMEM((count, rows, fd), F32)], 1
    )[0]


def last_blocks(index, blocks, rows, count):
    lanes = blocks[0].shape[1]
    n = count // lanes

    def body(index_ref, *refs):
        srcs, (out, a_ref, b_ref, c_ref) = refs[: len(blocks)], refs[len(blocks) :]
        sums = []
        for j, src in enumerate(srcs):
            x = src[...].astype(F32)
            at = pl.ds(pl.multiple_of(index_ref[j] * lanes, 128), lanes)
            out[:, at] = x[:rows, :]
            sums.append(x[rows : rows + n, :] + x[rows + n : rows + 2 * n, :])
        while len(sums) > 1:
            sums = [sums[i] + sums[i + 1] for i in range(0, len(sums), 2)]
        third = (n - 1) // 2
        a_ref[...] = sums[0][:third]
        b_ref[...] = sums[0][third : 2 * third]
        c_ref[...] = sums[0][2 * third :]

    third = (n - 1) // 2
    return kernel_call(
        body,
        [
            ((rows, len(blocks) * lanes), F32),
            ((third, lanes), F32),
            ((third, lanes), F32),
            ((1, lanes), F32),
        ],
        [index, *blocks],
        (),
        1,
    )


def local(
    block_input,
    norm1_gain,
    query_weight,
    key_weight,
    value_weight,
    query_gain,
    key_gain,
    output_weight,
    norm2_gain,
    w_gate,
    w_up,
    w_down,
    segments,
    positions,
    cotangent,
):
    rows, cols, dps = (lax.axis_size(a) for a in ("row", "col", "dp"))
    ri, ci, di = (lax.axis_index(a) for a in ("row", "col", "dp"))
    own, part = block_input.shape
    tokens = segments.shape[0]
    width = part * cols
    group = QUERY_HEADS // KEYVALUE_HEADS

    def cut(array, index, size, axis):
        return lax.dynamic_slice_in_dim(array, index * size, size, axis)

    order = rel_order(cols)

    order = rel_order(cols)

    def both_tokens(mine):
        return mine, swap(mine, "row", 1)

    def in_rel(blocks):
        return [blocks[o] for o in order]

    hq = query_weight.shape[1] // cols
    hk = key_weight.shape[1] // cols
    fd = w_gate.shape[1] // dps
    fs = fd // cols
    gate_up = [cut(w_gate, di, fd, 1).T, cut(w_up, di, fd, 1).T]
    down = cut(w_down, di, fd, 0)
    wq = output_weight.shape[0] // dps
    wo_piece = cut(output_weight, di, wq, 0)

    def qkv_for(k):
        return jnp.concatenate(
            [
                cut(query_weight, ci ^ k, hq, 1),
                cut(key_weight, ci ^ k, hk, 1),
                cut(value_weight, ci ^ k, hk, 1),
            ],
            1,
        )

    g1h, g1l = split_high(norm1_gain)
    g2h, g2l = split_high(norm2_gain)
    gain_rows = jnp.pad(jnp.stack([g1h, g1l, g2h, g2l]), ((0, 12), (0, 0)))
    got = gather_cols(jnp.concatenate([block_input, gain_rows], 0))
    x_pair = both_tokens(got[:own])
    x_all = jnp.concatenate(x_pair, 0)
    gains = got[own : own + 4].astype(F32)
    gain1 = gains[0] + gains[1]
    gain2 = gains[2] + gains[3]

    xf = x_all.astype(F32)
    inv1 = lax.rsqrt(jnp.mean(xf * xf, -1, keepdims=True) + EPS)
    xn = (xf * inv1 * gain1).astype(BF16)

    sent = [qkv_for(k) for k in range(cols)]
    back = exchange(sent, "col")
    qkv_came = back
    sent = [
        jnp.concatenate([wo_piece] + [cut(w, ci ^ k, fs, 0) for w in (down, *gate_up)], 0)
        for k in range(cols)
    ]
    came = exchange(sent, "col")

    back = after(came, xn)
    piece = jnp.stack(in_rel(back)[1:])
    wqkv = jnp.concatenate(in_rel(after(qkv_came, piece)), 0)

    def own_hidden(w):
        return lax.dynamic_index_in_dim(
            w.reshape(part, dps, cols, fs), ci, 2, False
        ).reshape(part, dps * fs).T

    own_down = lax.dynamic_index_in_dim(
        w_down.reshape(dps, cols, fs, part), ci, 1, False
    ).reshape(dps * fs, part)
    mine = [own_hidden(w_gate), own_hidden(w_up), own_down]

    def turn(index):
        out = jnp.zeros_like(index)
        bit, back_bit = 1, cols // 2
        while back_bit:
            out = out + jnp.where((index & bit) != 0, back_bit, 0)
            bit, back_bit = bit * 2, back_bit // 2
        return out

    each = jnp.arange(cols, dtype=jnp.int32)
    wc = output_weight.shape[0] // cols
    index = jnp.concatenate([(di ^ each) * fs, turn(ci ^ di ^ each) * wq, turn(ci ^ each) * wc])
    own_heads = cut(output_weight, ci, wc, 0)
    relayed = dps == cols == 4
    if relayed:
        near1 = swap(piece, "dp", 1)
        near2 = swap(piece, "dp", 2)
        relays = (near1[:, wq + fs :], near2[:, : wq + fs])
        far_gu = swap(relays[0], "dp", 2)
        far_wd = swap(relays[1], "dp", 1)
        pieces = [piece, near1, near2, far_gu, far_wd]
        wo_pieces = [piece, near1, near2, far_wd]
        which = (ci ^ di) & 3
        heads_rest = jnp.where(
            which < 2,
            jnp.where(which == 0, piece[:, :wq], near1[:, :wq]),
            jnp.where(which == 2, near2[:, :wq], far_wd[:, :wq]),
        )
        heads_rest = jnp.concatenate(list(heads_rest), 1)
    else:
        relays = ()
        stack = lax.all_gather(jnp.concatenate(list(piece), 1), "dp")
        pieces = [
            stack[:, wq + i * fs : wq + (i + 1) * fs].reshape(dps * fs, -1) for i in (1, 2, 0)
        ]
        wo_rows = stack[:, :wq].reshape(cols, wc, -1)
        wo_pieces = [
            jnp.concatenate(
                [lax.dynamic_index_in_dim(wo_rows, ci ^ k, 0, False) for k in order], 0
            )
        ]
        heads_rest = wo_pieces[0][:wc]
    wo_heads = jnp.concatenate([own_heads, heads_rest], 1)

    qkv = nn(xn, wqkv)
    kv = hk // HEAD_SIZE
    q = qkv[:, :hq].reshape(tokens, kv, group, HEAD_SIZE)
    k = qkv[:, hq : hq + hk].reshape(tokens, kv, HEAD_SIZE)
    vb = qkv[:, hq + hk :].astype(BF16).reshape(tokens, kv, HEAD_SIZE)
    rq = lax.rsqrt(jnp.mean(q * q, -1, keepdims=True) + EPS)
    rk = lax.rsqrt(jnp.mean(k * k, -1, keepdims=True) + EPS)
    qn = q * rq * query_gain
    kn = k * rk * key_gain

    def relative(vec):
        return jnp.concatenate([cut(vec, ri ^ j, own, 0) for j in range(rows)], 0)

    where = relative(jnp.arange(tokens, dtype=jnp.int32))
    segs = relative(segments)
    cosine, sine = rope_tables(relative(positions))
    cq, sq = cosine[:, None, None, :], sine[:, None, None, :]
    ck, sk = cosine[:, None, :], sine[:, None, :]
    qb = (qn * cq + rotate_forward(qn) * sq).astype(BF16)
    kb = (kn * ck + rotate_forward(kn) * sk).astype(BF16)
    allowed = (
        (segs[:, None] == segs[None, :])
        & (where[None, :] <= where[:, None])
        & (where[None, :] // SEQUENCE_TOKENS == where[:, None] // SEQUENCE_TOKENS)
    )
    scale = HEAD_SIZE ** (-0.5)
    score = jnp.einsum("qkgd,skd->kgqs", qb, kb, preferred_element_type=F32) * scale
    score = jnp.where(allowed, score, -jnp.inf)
    peak = jnp.max(score, -1, keepdims=True)
    lse = jnp.log(jnp.sum(jnp.exp(score - peak), -1, keepdims=True)) + peak
    prob = jnp.exp(score - lse)
    pb = prob.astype(BF16)
    ob = jnp.einsum("kgqs,skd->qkgd", pb, vb, preferred_element_type=F32).astype(BF16)
    ob = ob.reshape(tokens, hq)

    obs = gather_parts(ob, relays)
    obs[0] = after(obs[0], obs[1])
    mixed, mixed_b = project(index, obs, output_weight, wo_pieces, wq, not relayed)
    cot_pair = both_tokens(gather_cols(cotangent, (obs[1], mixed_b)))
    (dn_keep, dn_row, dn_msg, rs_keep, rs_msg, hid, dgb, dub, hn, h1_own, inv2_own, g2_part) = (
        feed_forward(
            index,
            x_pair,
            mixed,
            swap(mixed_b, "row", 1),
            mine,
            pieces,
            cot_pair,
            gain2[None],
            (own, fs, part),
        )
    )
    dn_total, dn_sent = owners(dn_keep, dn_row[:1], dn_msg)
    dhn, u2h = dn_total()
    hid, rs_keep, rs_msg = after((hid, rs_keep, rs_msg), dn_sent)
    dh1 = (
        cotangent.astype(F32)
        + inv2_own * (dhn * norm2_gain)
        - h1_own * (inv2_own * inv2_own * inv2_own) * (u2h[0][:, None] / width)
    )
    dh1b = dh1.astype(BF16)
    dh_cols = gather_direct(dh1b)
    dh1_all = jnp.concatenate(both_tokens(dh_cols), 0)

    def to_cols(array):
        blocks = [None] * cols
        for i, o in enumerate(order):
            blocks[o] = array[:, i * part : (i + 1) * part]
        return exchange(blocks, "col")

    do = nt(dh1_all, wo_heads)
    delta = jnp.sum((do * ob.astype(F32)).reshape(tokens, kv, group, HEAD_SIZE), -1)
    dob = do.astype(BF16).reshape(tokens, kv, group, HEAD_SIZE)
    dp = jnp.einsum("qkgd,skd->kgqs", dob, vb, preferred_element_type=F32)
    dsb = (prob * (dp - jnp.transpose(delta, (1, 2, 0))[..., None])).astype(BF16)
    dv = jnp.einsum("kgqs,qkgd->skd", pb, dob, preferred_element_type=F32)
    dqr = jnp.einsum("kgqs,skd->qkgd", dsb, kb, preferred_element_type=F32) * scale
    dkr = jnp.einsum("kgqs,qkgd->skd", dsb, qb, preferred_element_type=F32) * scale
    dqn = dqr * cq + rotate_backward(dqr * sq)
    dkn = dkr * ck + rotate_backward(dkr * sk)
    qg_part = jnp.sum(dqn * q * rq, (0, 1, 2))
    kg_part = jnp.sum(dkn * k * rk, (0, 1))
    uq = dqn * query_gain
    uk = dkn * key_gain
    dq = rq * uq - q * (rq * rq * rq) * jnp.mean(uq * q, -1, keepdims=True)
    dk = rk * uk - k * (rk * rk * rk) * jnp.mean(uk * k, -1, keepdims=True)
    dqkv = jnp.concatenate(
        [dq.reshape(tokens, hq), dk.reshape(tokens, hk), dv.reshape(tokens, hk)], 1
    ).astype(BF16)

    dxn_part = nt(dqkv, wqkv)
    u1x = jnp.sum(dxn_part * gain1 * xf, -1)[None]
    g1_part = jnp.sum(dxn_part * xf * inv1, 0, keepdims=True)
    dx_total, dx_sent = owners(dxn_part[:own], u1x[:, :own], packed(dxn_part[own:], u1x[:, own:]))
    rs_total, _ = owners(rs_keep, None, rs_msg)

    def features_first(left, right):
        return tn(left, right).astype(BF16).reshape(cols, dps, part // dps, right.shape[1])

    def by_rel(blocks):
        out = [None] * cols
        for i, o in enumerate(order):
            out[o] = blocks[i]
        return out

    def in_order(vec):
        return jnp.concatenate(
            [cut(vec, turn(ci ^ j), part, 0) for j in range(cols)], 0
        )

    vec = jnp.concatenate([in_order(g1_part[0]), in_order(g2_part[0]), qg_part, kg_part])
    vec = vec + swap(vec, "row", 1)
    count = vec.shape[0]
    assert count == 17 * hq and hq == 2 * HEAD_SIZE

    def halves(vec, lanes):
        flat = jnp.concatenate(split_high(vec))
        rows_needed = -(-flat.shape[0] // (16 * lanes)) * 16
        return jnp.pad(flat, (0, rows_needed * lanes - flat.shape[0])).reshape(rows_needed, lanes)

    def total(blocks):
        sums = [b.astype(F32).reshape(-1) for b in blocks]
        sums = [x[:count] + x[count : 2 * count] for x in sums]
        while len(sums) > 1:
            sums = [sums[i] + sums[i + 1] for i in range(0, len(sums), 2)]
        return sums[0]

    m = dps // cols
    full = tn(*after((xn, dqkv), dx_sent)).astype(BF16)
    go_full = features_first(dh1_all, ob)

    def qkv_piece(j):
        block = cut(full, turn((j // m) ^ ci), part, 0)
        if m == 1:
            return block
        return jnp.concatenate(
            [
                cut(block[:, :hq], j % m, hq // m, 1),
                cut(block[:, hq : hq + hk], j % m, hk // m, 1),
                cut(block[:, hq + hk :], j % m, hk // m, 1),
            ],
            1,
        )

    def out_piece(j):
        return lax.dynamic_index_in_dim(go_full, j, 1, False).reshape(-1, hq)

    if dps == cols:
        lanes = hq + part
        extra = halves(vec, lanes)
        got = exchange(
            [
                jnp.concatenate([jnp.concatenate([out_piece(di ^ k), qkv_piece(di ^ k)], 1), extra], 0)
                for k in range(dps)
            ],
            "dp",
        )
        got = after(got, dx_sent)
        both = sum(g[:part].astype(F32) for g in got).astype(BF16)
        go_mine, gq_mine = both[:, :hq], both[:, hq:]
        vec = total([g[part:] for g in got])
    else:
        go_mine = dp_scatter(out_piece).astype(BF16)
        gq_mine = dp_scatter(qkv_piece).astype(BF16)
        vec = lax.psum(vec, "dp")
    g_qkv = lax.ppermute(
        gq_mine,
        ("dp", "col"),
        [(p * cols + c, (c * m + p % m) * cols + p // m) for p in range(dps) for c in range(cols)],
    ).astype(F32)
    g_query = g_qkv[:, : hq // m]
    g_key = g_qkv[:, hq // m : (hq + hk) // m]
    g_value = g_qkv[:, (hq + hk) // m :]

    blocks = by_rel(go_mine.reshape(cols, part // dps, hq))
    extra = halves(vec, hq)
    goz_sent = [jnp.concatenate([b, extra], 0) for b in blocks]
    goz_got = exchange(goz_sent, "col")

    g_full = [tn(d, hn).astype(BF16) for d in (dgb, dub)]

    def gu_piece(j):
        return jnp.concatenate([cut(g, j, fs, 0) for g in g_full], 0)

    mine = dp_scatter(gu_piece, dh_cols).astype(BF16)
    back = after(to_cols(mine), dx_sent)
    result = (h1_own + rs_total(goz_sent)[0]).astype(BF16)
    g_gate, g_up = (g.T for g in gate_up_blocks(ci ^ each, back, fs))

    gd_full = features_first(jnp.concatenate(cot_pair, 0), hid)

    def gd_piece(j):
        return lax.dynamic_index_in_dim(gd_full, j, 1, False)

    mine = dp_scatter(gd_piece, dx_sent).astype(BF16)
    back = after(exchange(by_rel(mine), "col"), goz_sent)
    g_down = feature_blocks(ci ^ each, back, fs, dps).T

    dxn, u1x = dx_total(goz_sent)
    inv1_own = inv1[:own]
    d_input = (
        dh1
        + inv1_own * (dxn * norm1_gain)
        - block_input.astype(F32) * (inv1_own * inv1_own * inv1_own) * (u1x[0][:, None] / width)
    )

    g_out, g_norm1, g_norm2, head_gains = last_blocks(ci ^ each, goz_got, part // dps, count)
    g_out = g_out.T
    g_norm1 = g_norm1.reshape(width)
    g_norm2 = g_norm2.reshape(width)
    g_qgain = head_gains[0, :HEAD_SIZE]
    g_kgain = head_gains[0, HEAD_SIZE:]
    return (
        result,
        d_input,
        g_norm1,
        g_query,
        g_key,
        g_value,
        g_qgain,
        g_kgain,
        g_out,
        g_norm2,
        g_gate,
        g_up,
        g_down,
    )


def solution(mesh):
    in_specs = (
        P(("dp", "row"), "col"),
        P("col"),
        P("col", "row"),
        P("col", "row"),
        P("col", "row"),
        P(),
        P(),
        P("row", "col"),
        P("col"),
        P("col", "row"),
        P("col", "row"),
        P("row", "col"),
        P("dp"),
        P("dp"),
        P(("dp", "row"), "col"),
    )
    out_specs = (
        P(("dp", "row"), "col"),
        P(("dp", "row"), "col"),
        P(),
        P("col", ("row", "dp")),
        P("col", ("row", "dp")),
        P("col", ("row", "dp")),
        P(),
        P(),
        P("row", ("col", "dp")),
        P(),
        P("col", ("row", "dp")),
        P("col", ("row", "dp")),
        P("row", ("col", "dp")),
    )

    return jax.shard_map(local, mesh=mesh, in_specs=in_specs, out_specs=out_specs, check_vma=False)
```
